32 devices in a mesh: dp: 8 (over z, x), ctx: 4 (over y, core).
Axes of the slice: x: 2, y: 2, z: 4, core: 2. Of those that a mesh axis runs over, the one named last changes fastest.
Arguments:
- tokens: bfloat16 [32, 2560, 1280], P('dp', 'ctx'), may hold values from -64 to 64
- router: bfloat16 [1280, 64], replicated, may hold values from -1 to 1
- expert_up: bfloat16 [32, 1280, 2560], P(('dp', 'ctx')), may hold values from -0.5 to 0.5
- expert_down: bfloat16 [32, 2560, 1280], P(('dp', 'ctx')), may hold values from -0.25 to 0.25
Outputs:
- mixed: bfloat16 [32, 2560, 1280], P('dp', 'ctx')
The draws below stay inside these ranges and needn't reach their ends.
All inputs are finite; a program needn't handle non-finite values.
Results may differ from the reference program's by a relative error of at most 0.015.
Values may be sent and summed in bfloat16 or wider, within the bound.
A program may use at most 128 MiB of HBM per device.

```python
import math
import jax
import jax.numpy as jnp
from jax import lax

D = 1280
FF = 2560
PER_EXPERT = 2
TOK_DEV = 640
EXPERTS = 32
SLOTS = 64
CLIPS = 32
TOK = 2560
N_CTX = 4


def router_table(key):
    normal_draw = jax.random.normal(jax.random.fold_in(key, 7), (D, SLOTS), jnp.float32)
    lengths = jnp.sqrt(jnp.sum(normal_draw * normal_draw, axis=0))
    target = jnp.exp(jax.random.uniform(jax.random.fold_in(key, 8), (SLOTS,), jnp.float32, math.log(2.2), math.log(3.2)))
    return jnp.clip(normal_draw / lengths[None, :] * target[None, :], -1.0, 1.0)


def draw_router(key, part):
    return router_table(key).astype(jnp.bfloat16)


def draw_tokens(key, part):
    values = jnp.clip(jax.random.normal(jax.random.fold_in(key, 1), (CLIPS, TOK, D), jnp.float32), -6.0, 6.0)
    return values.astype(jnp.bfloat16)


def block_levels(key, dims, pieces, smallest, largest):
    def one(dim, blocks):
        steps = jax.random.uniform(jax.random.fold_in(jax.random.fold_in(key, 6), dim), (blocks,), jnp.float32, smallest / len(pieces), largest / len(pieces))
        return jnp.repeat(jnp.exp(steps), dims[dim] // blocks).reshape((-1,) + (1,) * (len(dims) - dim - 1))

    factor_of = one(*pieces[0])
    for cut in pieces[1:]:
        factor_of = factor_of * one(*cut)
    return factor_of


def noise(rng, shape, spread, bound, split=(), dtype=jnp.bfloat16):
    values = spread * jax.random.normal(rng, shape, jnp.float32)
    if split:
        values = values * block_levels(rng, shape, split, -0.22, 0.18)
    return jnp.clip(values, -bound, bound).astype(dtype)


def setup_inputs(seed: int = 0) -> dict:
    keys = jax.random.split(jax.random.key(seed), 5)
    tokens = draw_tokens(jax.random.fold_in(keys[4], 71), 0)
    router = draw_router(jax.random.fold_in(keys[4], 71), 0)
    expert_up = noise(keys[2], (EXPERTS, D, FF), (D // 9) ** -0.5, 0.5, ((0, 32),))
    expert_down = noise(keys[3], (EXPERTS, FF, D), (FF // 4) ** -0.5, 0.25, ((0, 32),))
    return {"tokens": tokens, "router": router, "expert_up": expert_up, "expert_down": expert_down}


def reference(tokens, router, expert_up, expert_down):
    def per_clip(clip_rows):
        logits = jnp.dot(clip_rows, router, preferred_element_type=jnp.float32)
        column_max = jnp.max(logits, axis=0)
        exponent = jnp.exp(logits - column_max[None, :])
        dispatch = (exponent / jnp.sum(exponent, axis=0)[None, :]).astype(jnp.bfloat16)
        blocks = jnp.einsum("btj,btd->bjd", dispatch.reshape(N_CTX, TOK_DEV, SLOTS).astype(jnp.float32), clip_rows.reshape(N_CTX, TOK_DEV, D).astype(jnp.float32))
        blocks = lax.optimization_barrier(blocks.astype(jnp.bfloat16)).astype(jnp.float32)
        slot_inputs = jnp.sum(blocks, axis=0).astype(jnp.bfloat16)
        row_max = jnp.max(logits, axis=1)
        row_exp = jnp.exp(logits - row_max[:, None])
        combine = (row_exp / jnp.sum(row_exp, axis=1)[:, None]).astype(jnp.bfloat16)
        return slot_inputs, combine

    slot_inputs, combine = lax.map(per_clip, tokens)
    grouped = jnp.moveaxis(slot_inputs.reshape(CLIPS, EXPERTS, PER_EXPERT, D), 1, 0)

    def per_expert(bundle):
        slot_rows, up_matrix, down_matrix = bundle
        flat = slot_rows.reshape(CLIPS * PER_EXPERT, D)
        hidden = jax.nn.gelu(jnp.dot(flat, up_matrix, preferred_element_type=jnp.float32), approximate=False).astype(jnp.bfloat16)
        produced = jnp.dot(hidden, down_matrix, preferred_element_type=jnp.float32).astype(jnp.bfloat16)
        return produced.reshape(CLIPS, PER_EXPERT, D)

    produced = lax.map(per_expert, (grouped, expert_up, expert_down))
    slot_outputs = jnp.moveaxis(produced, 0, 1).reshape(CLIPS, SLOTS, D)

    def per_mix(bundle):
        return jnp.dot(bundle[0], bundle[1], preferred_element_type=jnp.float32).astype(jnp.bfloat16)

    return lax.map(per_mix, (combine, slot_outputs))
```

```python
import functools

import jax
import jax.numpy as jnp
import numpy as np
from jax import lax
from jax.experimental import pallas as pl
from jax.experimental.pallas import tpu as pltpu
from jax.sharding import PartitionSpec as P

MESH = pl.DeviceIdType.MESH
CORES = 2
F32 = jnp.float32
BF16 = jnp.bfloat16


def clip_rows(shape, clip, per_clip, group):
    place = lax.rem(lax.broadcasted_iota(jnp.int32, shape, 0), group)
    return (place >= clip * per_clip) & (place < (clip + 1) * per_clip)


def exchange(
    dims, tok_hbm, router_ref, spread_ref, up_hbm, down_hbm, gathered_ref, combine_ref,
    tok, up, down, logit, diag, acc, part, from_core, chip, from_y, slab, rows_in, result, pool,
    stat, stats_in,
    tok_sem, weight_sem, stat_sem, core_sem, y_sem, dp_sem, back_sem, ysend_sem, csend_sem,
):
    n_dp, n_ctx, clips, tok_dev, per_expert, chunks, width = dims
    n_y = n_ctx // CORES
    group = clips * per_expert
    rows = n_dp * n_ctx * group
    dp = lax.axis_index("dp")
    ctx = lax.axis_index("ctx")
    y = ctx // CORES
    core = ctx % CORES
    other = 1 - core

    token_copies = []
    for c in range(clips):
        copy = pltpu.make_async_copy(tok_hbm.at[c], tok.at[pl.ds(c * tok_dev, tok_dev)], tok_sem.at[c])
        copy.start()
        token_copies.append(copy)
    up_copy = pltpu.make_async_copy(up_hbm.at[0], up, weight_sem.at[0])
    up_copy.start()
    down_copy = pltpu.make_async_copy(down_hbm.at[0], down, weight_sem.at[1])
    down_copy.start()

    barrier = pltpu.get_barrier_semaphore()
    for k in range(1, n_ctx):
        pl.semaphore_signal(barrier, inc=1, device_id=(dp, (ctx + k) % n_ctx), device_id_type=MESH)
    for k in range(1, n_dp):
        pl.semaphore_signal(barrier, inc=1, device_id=((dp + k) % n_dp, ctx), device_id_type=MESH)

    def send(src, dst, sems, index, target):
        copy = pltpu.make_async_remote_copy(
            src_ref=src, dst_ref=dst, send_sem=sems.at[(0,) + index], recv_sem=sems.at[(1,) + index],
            device_id=target, device_id_type=MESH,
        )
        copy.start()
        return copy

    routed = jnp.dot(spread_ref[...], router_ref[...], preferred_element_type=F32).astype(BF16)
    for c in range(clips):
        token_copies[c].wait()
        here = lax.dot_general(
            routed, tok[pl.ds(c * tok_dev, tok_dev), :], (((1,), (1,)), ((), ())), preferred_element_type=F32
        )
        if c == 0:
            logit[...] = here
        else:
            logit[...] = jnp.where(clip_rows((rows, tok_dev), c, per_expert, group), here, logit[...])
    highest = jnp.max(logit[...], axis=1, keepdims=True)
    powers = jnp.exp(logit[...] - highest)
    total = jnp.sum(powers, axis=1, keepdims=True)
    lane = lax.broadcasted_iota(jnp.int32, (rows, 128), 1)
    stat[...] = jnp.where(lane == 0, highest, total).T[0:8, :]
    pl.semaphore_wait(barrier, n_ctx - 1 + n_dp - 1)
    stat_copies = [
        send(stat, stats_in.at[k - 1], stat_sem, (k - 1,), (dp, (ctx + k) % n_ctx)) for k in range(1, n_ctx)
    ]
    for c in range(clips):
        diag[:, pl.ds(c * tok_dev, tok_dev)] = jnp.where(
            clip_rows((rows, tok_dev), c, per_expert, group), powers, 0.0
        ).astype(BF16)

    started = []

    def block_sums(f):
        return jnp.dot(diag[...], tok[:, pl.ds(f * width, width)], preferred_element_type=F32)

    def first(f, value, scale):
        value = (value * scale).reshape(CORES, n_y, n_dp, group, width)
        part[f] = value.astype(BF16)
        copy = send(part.at[f, other], from_core.at[f], core_sem, (f,), (dp, y * CORES + other))
        return copy

    def second(f, copy):
        copy.wait_recv()
        chip[f] = (part[f, core].astype(F32) + from_core[f].astype(F32)).astype(BF16)
        copies = []
        for k in range(1, n_y):
            there = (y + k) % n_y
            copies.append(
                send(chip.at[f, there], from_y.at[f, k - 1], y_sem, (f, k - 1), (dp, there * CORES + core))
            )
        return copies

    def third(f, copies):
        value = chip[f, y].astype(F32)
        for k in range(1, n_y):
            copies[k - 1].wait_recv()
            value = value + from_y[f, k - 1].astype(F32)
        slab[f] = value.astype(BF16)
        rows_in[f, dp] = slab[f, dp]
        return [
            send(slab.at[f, (dp + k) % n_dp], rows_in.at[f, dp], dp_sem, (f, k - 1), ((dp + k) % n_dp, ctx))
            for k in range(1, n_dp)
        ]

    def fourth(f, copies):
        for copy in copies:
            copy.wait_recv()
        value = rows_in[f].astype(F32).reshape(n_dp * group, width).astype(BF16)
        term = jnp.dot(value, up[pl.ds(f * width, width), :], preferred_element_type=F32)
        acc[...] = term if f == 0 else acc[...] + term

    opening = block_sums(0)
    for copy in stat_copies:
        copy.wait_recv()
    best, amount = stat[0:1, :], stat[1:2, :]
    top = best
    for k in range(1, n_ctx):
        top = jnp.maximum(top, stats_in[k - 1, 0:1, :])
    whole = amount * jnp.exp(best - top)
    for k in range(1, n_ctx):
        whole = whole + stats_in[k - 1, 1:2, :] * jnp.exp(stats_in[k - 1, 0:1, :] - top)
    scale = jnp.broadcast_to(jnp.exp(best - top) / whole, (128, rows)).T[:, 0:1]

    one, two, three = {}, {}, {}
    for t in range(chunks + 2):
        if t < chunks:
            one[t] = first(t, opening if t == 0 else block_sums(t), scale)
        if 0 <= t - 1 < chunks:
            two[t - 1] = second(t - 1, one[t - 1])
        if 0 <= t - 2 < chunks:
            three[t - 2] = third(t - 2, two[t - 2])

    blocks = logit[...].reshape(rows // group, group, tok_dev)
    peak = jnp.max(blocks, axis=0)

    def over_slots(values, reduce, neutral):
        out = values
        for c in range(clips):
            mine = clip_rows((group, tok_dev), c, per_expert, group)
            out = jnp.where(mine, reduce(jnp.where(mine, values, neutral), axis=0, keepdims=True), out)
        return out

    peak = over_slots(peak, jnp.max, -jnp.inf)
    powers = jnp.exp(blocks - peak[None])
    norm = over_slots(jnp.sum(powers, axis=0), jnp.sum, 0.0)
    combine_ref[...] = (powers / norm[None]).reshape(rows, tok_dev).astype(BF16)

    up_copy.wait()
    for f in range(chunks):
        fourth(f, three[f])
    value = acc[...]
    hidden = (0.5 * value * (1.0 + lax.erf(value * np.float32(np.sqrt(0.5))))).astype(BF16)
    down_copy.wait()

    def fifth(f):
        value = jnp.dot(hidden, down[:, pl.ds(f * width, width)], preferred_element_type=F32)
        result[f] = value.reshape(n_dp, group, width).astype(BF16)
        pool[f, core, y, dp] = result[f, dp]
        return [
            send(
                result.at[f, (dp + k) % n_dp], pool.at[f, core, y, dp], back_sem, (f, k - 1),
                ((dp + k) % n_dp, ctx),
            )
            for k in range(1, n_dp)
        ]

    def sixth(f, copies):
        for copy in copies:
            copy.wait_recv()
        piece = pool.at[f, core, y]
        beyond = [
            send(piece, piece, ysend_sem, (f, k - 1), (dp, ((y + k) % n_y) * CORES + core)) for k in range(1, n_y)
        ]
        across = [send(piece, piece, csend_sem, (f, 0), (dp, y * CORES + other))]
        return beyond, across

    def seventh(f, copies):
        beyond, across = copies
        for k in range(1, n_y):
            beyond[k - 1].wait_recv()
            piece = pool.at[f, core, (y + n_y - k) % n_y]
            across.append(send(piece, piece, csend_sem, (f, k), (dp, y * CORES + other)))
        return across

    five, six, seven = {}, {}, {}
    for t in range(chunks + 2):
        if t < chunks:
            five[t] = fifth(t)
        if 0 <= t - 1 < chunks:
            six[t - 1] = sixth(t - 1, five[t - 1])
        if 0 <= t - 2 < chunks:
            seven[t - 2] = seventh(t - 2, six[t - 2])
    for f in range(chunks):
        for copy in seven[f]:
            copy.wait_recv()
        gathered_ref[f] = pool[f].astype(F32).reshape(rows, width).astype(BF16)

    for copy in stat_copies:
        copy.wait_send()
    for f in range(chunks):
        for copy in [one[f]] + two[f] + three[f] + five[f] + six[f][0] + seven[f]:
            copy.wait_send()


def mix(clips, per_expert, chunks, width, combine_ref, gathered_ref, out_ref):
    group = clips * per_expert
    mine = clip_rows(combine_ref.shape, pl.program_id(0), per_expert, group)
    weights = jnp.where(mine, combine_ref[...].astype(F32), 0.0).T.astype(BF16)
    for f in range(chunks):
        out_ref[0, :, pl.ds(f * width, width)] = jnp.dot(
            weights, gathered_ref[f], preferred_element_type=F32
        ).astype(BF16)


def shards(n_dp, n_ctx, tokens, router, expert_up, expert_down):
    clips, tok_dev, feature = tokens.shape
    slots = router.shape[1]
    hidden = expert_up.shape[2]
    per_expert = slots // (n_dp * n_ctx)
    n_y = n_ctx // CORES
    group = clips * per_expert
    rows = n_dp * n_ctx * group
    width = 256
    chunks = feature // width
    order = np.arange(slots).reshape(n_dp, n_y, CORES, 1, per_expert).transpose(2, 1, 0, 3, 4)
    order = np.broadcast_to(order, (CORES, n_y, n_dp, clips, per_expert)).reshape(-1)
    spread = jnp.asarray(order[:, None] == np.arange(slots)[None, :], BF16)
    dims = (n_dp, n_ctx, clips, tok_dev, per_expert, chunks, width)
    vmem = pl.BlockSpec(memory_space=pltpu.VMEM)
    hbm = pl.BlockSpec(memory_space=pl.ANY)
    piece = (n_dp, group, width)
    dma = pltpu.SemaphoreType.DMA
    gathered, combine = pl.pallas_call(
        functools.partial(exchange, dims),
        out_shape=(
            jax.ShapeDtypeStruct((chunks, rows, width), BF16),
            jax.ShapeDtypeStruct((rows, tok_dev), BF16),
        ),
        in_specs=[hbm, vmem, vmem, hbm, hbm],
        out_specs=(vmem, vmem),
        scratch_shapes=[
            pltpu.VMEM((clips * tok_dev, feature), BF16),
            pltpu.VMEM((feature, hidden), BF16),
            pltpu.VMEM((hidden, feature), BF16),
            pltpu.VMEM((rows, tok_dev), F32),
            pltpu.VMEM((rows, clips * tok_dev), BF16),
            pltpu.VMEM((n_dp * group, hidden), F32),
            pltpu.VMEM((chunks, CORES, n_y) + piece, BF16),
            pltpu.VMEM((chunks, n_y) + piece, BF16),
            pltpu.VMEM((chunks, n_y) + piece, BF16),
            pltpu.VMEM((chunks, n_y - 1) + piece, BF16),
            pltpu.VMEM((chunks,) + piece, BF16),
            pltpu.VMEM((chunks,) + piece, BF16),
            pltpu.VMEM((chunks,) + piece, BF16),
            pltpu.VMEM((chunks, CORES, n_y) + piece, BF16),
            pltpu.VMEM((8, rows), F32),
            pltpu.VMEM((n_ctx - 1, 8, rows), F32),
            dma((clips,)),
            dma((2,)),
            dma((2, n_ctx - 1)),
            dma((2, chunks)),
            dma((2, chunks, n_y - 1)),
            dma((2, chunks, n_dp - 1)),
            dma((2, chunks, n_dp - 1)),
            dma((2, chunks, n_y - 1)),
            dma((2, chunks, n_y)),
        ],
        compiler_params=pltpu.CompilerParams(collective_id=0, has_side_effects=True),
        name="exchange",
    )(tokens, router.T, spread, expert_up, expert_down)
    return pl.pallas_call(
        functools.partial(mix, clips, per_expert, chunks, width),
        grid=(clips,),
        out_shape=jax.ShapeDtypeStruct(tokens.shape, BF16),
        in_specs=[
            pl.BlockSpec((rows, tok_dev), lambda c: (0, 0)),
            pl.BlockSpec((chunks, rows, width), lambda c: (0, 0, 0)),
        ],
        out_specs=pl.BlockSpec((1, tok_dev, feature), lambda c: (c, 0, 0)),
        name="mix",
    )(combine, gathered)


def solution(mesh):
    in_specs = (
        P("dp", "ctx", None),
        P(),
        P(("dp", "ctx"), None, None),
        P(("dp", "ctx"), None, None),
    )
    out_specs = P("dp", "ctx", None)
    body = functools.partial(shards, mesh.shape["dp"], mesh.shape["ctx"])
    return jax.shard_map(body, mesh=mesh, in_specs=in_specs, out_specs=out_specs, check_vma=False)
```

```python
import functools

import jax
import jax.numpy as jnp
import numpy as np
from jax import lax
from jax.experimental import pallas as pl
from jax.experimental.pallas import tpu as pltpu
from jax.sharding import PartitionSpec as P

MESH = pl.DeviceIdType.MESH
CORES = 2
LAG = 4
F32 = jnp.float32
BF16 = jnp.bfloat16


def clip_rows(shape, clip, per_clip, group, dim=0):
    place = lax.rem(lax.broadcasted_iota(jnp.int32, shape, dim), group)
    return (place >= clip * per_clip) & (place < (clip + 1) * per_clip)


def exchange(
    dims, tok_hbm, router_ref, spread_ref, up_hbm, down_hbm, gathered_ref, combine_ref,
    tok, up, down, flipped, logit, diag, sums, acc, part, from_core, chip, from_y, slab, rows_in, result, pool,
    stat, stats_in,
    tok_sem, weight_sem, stat_sem, core_sem, y_sem, dp_sem, back_sem, ysend_sem, csend_sem,
):
    n_dp, n_ctx, clips, tok_dev, per_expert, chunks, width = dims
    n_y = n_ctx // CORES
    group = clips * per_expert
    rows = n_dp * n_ctx * group
    dp = lax.axis_index("dp")
    ctx = lax.axis_index("ctx")
    y = ctx // CORES
    core = ctx % CORES
    other = 1 - core

    token_copies = []
    for c in range(clips):
        copy = pltpu.make_async_copy(tok_hbm.at[c], tok.at[pl.ds(c * tok_dev, tok_dev)], tok_sem.at[c])
        copy.start()
        token_copies.append(copy)
    up_copy = pltpu.make_async_copy(up_hbm.at[0], up, weight_sem.at[0])
    up_copy.start()
    down_copy = pltpu.make_async_copy(down_hbm.at[0], down, weight_sem.at[1])
    down_copy.start()

    barrier = pltpu.get_barrier_semaphore()
    for k in range(1, n_ctx):
        pl.semaphore_signal(barrier, inc=1, device_id=(dp, (ctx + k) % n_ctx), device_id_type=MESH)
    for k in range(1, n_dp):
        pl.semaphore_signal(barrier, inc=1, device_id=((dp + k) % n_dp, ctx), device_id_type=MESH)

    def send(src, dst, sems, index, target):
        copy = pltpu.make_async_remote_copy(
            src_ref=src, dst_ref=dst, send_sem=sems.at[(0,) + index], recv_sem=sems.at[(1,) + index],
            device_id=target, device_id_type=MESH,
        )
        copy.start()
        return copy

    routed = jnp.dot(spread_ref[...], router_ref[...], preferred_element_type=F32).T.astype(BF16)
    for c in range(clips):
        token_copies[c].wait()
        here = jnp.dot(tok[pl.ds(c * tok_dev, tok_dev), :], routed, preferred_element_type=F32)
        if c == 0:
            flipped[...] = here
        else:
            flipped[...] = jnp.where(clip_rows((tok_dev, rows), c, per_expert, group, 1), here, flipped[...])
    logit[...] = flipped[...].T
    highest = jnp.max(logit[...], axis=1, keepdims=True)
    powers = jnp.exp(logit[...] - highest)
    total = jnp.sum(powers, axis=1, keepdims=True)
    lane = lax.broadcasted_iota(jnp.int32, (rows, 128), 1)
    stat[...] = jnp.where(lane == 0, highest, total).T[0:8, :]
    pl.semaphore_wait(barrier, n_ctx - 1 + n_dp - 1)
    stat_copies = [
        send(stat, stats_in.at[k - 1], stat_sem, (k - 1,), (dp, (ctx + k) % n_ctx)) for k in range(1, n_ctx)
    ]
    for c in range(clips):
        diag[:, pl.ds(c * tok_dev, tok_dev)] = jnp.where(
            clip_rows((rows, tok_dev), c, per_expert, group), powers, 0.0
        ).astype(BF16)

    def block_sums(f):
        return jnp.dot(diag[...], tok[:, pl.ds(f * width, width)], preferred_element_type=F32)

    def first(f, value, scale):
        value = (value * scale).reshape(CORES, n_y, n_dp, group, width)
        part[f] = value.astype(BF16)
        copy = send(part.at[f, other], from_core.at[f], core_sem, (f,), (dp, y * CORES + other))
        return copy

    def second(f, copy):
        copy.wait_recv()
        chip[f] = (part[f, core].astype(F32) + from_core[f].astype(F32)).astype(BF16)
        copies = []
        for k in range(1, n_y):
            there = (y + k) % n_y
            copies.append(
                send(chip.at[f, there], from_y.at[f, k - 1], y_sem, (f, k - 1), (dp, there * CORES + core))
            )
        return copies

    def third(f, copies):
        value = chip[f, y].astype(F32)
        for k in range(1, n_y):
            copies[k - 1].wait_recv()
            value = value + from_y[f, k - 1].astype(F32)
        slab[f] = value.astype(BF16)
        rows_in[f, dp] = slab[f, dp]
        return [
            send(slab.at[f, (dp + k) % n_dp], rows_in.at[f, dp], dp_sem, (f, k - 1), ((dp + k) % n_dp, ctx))
            for k in range(1, n_dp)
        ]

    def fourth(f, copies):
        for copy in copies:
            copy.wait_recv()
        value = rows_in[f].astype(F32).reshape(n_dp * group, width).astype(BF16)
        term = jnp.dot(value, up[pl.ds(f * width, width), :], preferred_element_type=F32)
        acc[...] = term if f == 0 else acc[...] + term

    for f in range(chunks):
        sums[f] = block_sums(f)
    for copy in stat_copies:
        copy.wait_recv()
    best, amount = stat[0:1, :], stat[1:2, :]
    top = best
    for k in range(1, n_ctx):
        top = jnp.maximum(top, stats_in[k - 1, 0:1, :])
    whole = amount * jnp.exp(best - top)
    for k in range(1, n_ctx):
        whole = whole + stats_in[k - 1, 1:2, :] * jnp.exp(stats_in[k - 1, 0:1, :] - top)
    scale = jnp.broadcast_to(jnp.exp(best - top) / whole, (128, rows)).T[:, 0:1]

    one, two, three = {}, {}, {}
    for t in range(chunks + LAG):
        if t < chunks:
            one[t] = first(t, sums[t], scale)
        if 0 <= t - 1 < chunks:
            two[t - 1] = second(t - 1, one[t - 1])
        if 0 <= t - LAG < chunks:
            three[t - LAG] = third(t - LAG, two[t - LAG])

    blocks = logit[...].reshape(rows // group, group, tok_dev)
    peak = jnp.max(blocks, axis=0)

    def over_slots(values, reduce, neutral):
        out = values
        for c in range(clips):
            mine = clip_rows((group, tok_dev), c, per_expert, group)
            out = jnp.where(mine, reduce(jnp.where(mine, values, neutral), axis=0, keepdims=True), out)
        return out

    peak = over_slots(peak, jnp.max, -jnp.inf)
    powers = jnp.exp(blocks - peak[None])
    norm = over_slots(jnp.sum(powers, axis=0), jnp.sum, 0.0)
    combine_ref[...] = (powers / norm[None]).reshape(rows, tok_dev).T.astype(BF16)

    up_copy.wait()
    for f in range(chunks):
        fourth(f, three[f])
    value = acc[...]
    hidden = (0.5 * value * (1.0 + lax.erf(value * np.float32(np.sqrt(0.5))))).astype(BF16)
    down_copy.wait()

    def fifth(f):
        value = jnp.dot(hidden, down[:, pl.ds(f * width, width)], preferred_element_type=F32)
        result[f] = value.reshape(n_dp, group, width).astype(BF16)
        pool[f, core, y, dp] = result[f, dp]
        return [
            send(
                result.at[f, (dp + k) % n_dp], pool.at[f, core, y, dp], back_sem, (f, k - 1),
                ((dp + k) % n_dp, ctx),
            )
            for k in range(1, n_dp)
        ]

    def sixth(f, copies):
        for copy in copies:
            copy.wait_recv()
        piece = pool.at[f, core, y]
        beyond = [
            send(piece, piece, ysend_sem, (f, k - 1), (dp, ((y + k) % n_y) * CORES + core)) for k in range(1, n_y)
        ]
        across = [send(piece, piece, csend_sem, (f, 0), (dp, y * CORES + other))]
        return beyond, across

    def seventh(f, copies):
        beyond, across = copies
        for k in range(1, n_y):
            beyond[k - 1].wait_recv()
            piece = pool.at[f, core, (y + n_y - k) % n_y]
            across.append(send(piece, piece, csend_sem, (f, k), (dp, y * CORES + other)))
        return across

    five, six, seven = {}, {}, {}
    for t in range(chunks):
        five[t] = fifth(t)
    for t in range(chunks + 2):
        if t < chunks:
            six[t] = sixth(t, five[t])
        if 0 <= t - 2 < chunks:
            seven[t - 2] = seventh(t - 2, six[t - 2])
    for f in range(chunks):
        for copy in seven[f]:
            copy.wait_recv()
        gathered_ref[f] = pool[f].astype(F32).reshape(rows, width).astype(BF16)

    for copy in stat_copies:
        copy.wait_send()
    for f in range(chunks):
        for copy in [one[f]] + two[f] + three[f] + five[f] + six[f][0] + seven[f]:
            copy.wait_send()


def mix(clips, per_expert, chunks, width, combine_ref, gathered_ref, out_ref):
    group = clips * per_expert
    mine = clip_rows(combine_ref.shape, pl.program_id(0), per_expert, group, 1)
    weights = jnp.where(mine, combine_ref[...].astype(F32), 0.0).astype(BF16)
    for f in range(chunks):
        out_ref[0, :, pl.ds(f * width, width)] = jnp.dot(
            weights, gathered_ref[f], preferred_element_type=F32
        ).astype(BF16)


def shards(n_dp, n_ctx, tokens, router, expert_up, expert_down):
    clips, tok_dev, feature = tokens.shape
    slots = router.shape[1]
    hidden = expert_up.shape[2]
    per_expert = slots // (n_dp * n_ctx)
    n_y = n_ctx // CORES
    group = clips * per_expert
    rows = n_dp * n_ctx * group
    width = 256
    parts = 1
    chunks = feature // width
    order = np.arange(slots).reshape(n_dp, n_y, CORES, 1, per_expert).transpose(2, 1, 0, 3, 4)
    order = np.broadcast_to(order, (CORES, n_y, n_dp, clips, per_expert)).reshape(-1)
    spread = jnp.asarray(order[:, None] == np.arange(slots)[None, :], BF16)
    dims = (n_dp, n_ctx, clips, tok_dev, per_expert, chunks, width)
    vmem = pl.BlockSpec(memory_space=pltpu.VMEM)
    hbm = pl.BlockSpec(memory_space=pl.ANY)
    piece = (n_dp, group, width)
    dma = pltpu.SemaphoreType.DMA
    gathered, combine = pl.pallas_call(
        functools.partial(exchange, dims),
        out_shape=(
            jax.ShapeDtypeStruct((chunks, rows, width), BF16),
            jax.ShapeDtypeStruct((tok_dev, rows), BF16),
        ),
        in_specs=[hbm, vmem, vmem, hbm, hbm],
        out_specs=(vmem, vmem),
        scratch_shapes=[
            pltpu.VMEM((clips * tok_dev, feature), BF16),
            pltpu.VMEM((feature, hidden), BF16),
            pltpu.VMEM((hidden, feature), BF16),
            pltpu.VMEM((tok_dev, rows), F32),
            pltpu.VMEM((rows, tok_dev), F32),
            pltpu.VMEM((rows, clips * tok_dev), BF16),
            pltpu.VMEM((chunks, rows, width), F32),
            pltpu.VMEM((n_dp * group, hidden), F32),
            pltpu.VMEM((chunks, CORES, n_y) + piece, BF16),
            pltpu.VMEM((chunks, n_y) + piece, BF16),
            pltpu.VMEM((chunks, n_y) + piece, BF16),
            pltpu.VMEM((chunks, n_y - 1) + piece, BF16),
            pltpu.VMEM((chunks,) + piece, BF16),
            pltpu.VMEM((chunks,) + piece, BF16),
            pltpu.VMEM((chunks,) + piece, BF16),
            pltpu.VMEM((chunks, CORES, n_y) + piece, BF16),
            pltpu.VMEM((8, rows), F32),
            pltpu.VMEM((n_ctx - 1, 8, rows), F32),
            dma((clips,)),
            dma((2,)),
            dma((2, n_ctx - 1)),
            dma((2, chunks)),
            dma((2, chunks, n_y - 1)),
            dma((2, chunks, n_dp - 1)),
            dma((2, chunks, n_dp - 1)),
            dma((2, chunks, n_y - 1)),
            dma((2, chunks, n_y)),
        ],
        compiler_params=pltpu.CompilerParams(collective_id=0, has_side_effects=True),
        name="exchange",
    )(tokens, router.T, spread, expert_up, expert_down)
    return pl.pallas_call(
        functools.partial(mix, clips, per_expert, chunks, width),
        grid=(clips, parts),
        out_shape=jax.ShapeDtypeStruct(tokens.shape, BF16),
        in_specs=[
            pl.BlockSpec((tok_dev // parts, rows), lambda c, t: (t, 0)),
            pl.BlockSpec((chunks, rows, width), lambda c, t: (0, 0, 0)),
        ],
        out_specs=pl.BlockSpec((1, tok_dev // parts, feature), lambda c, t: (c, t, 0)),
        name="mix",
    )(combine, gathered)


def solution(mesh):
    in_specs = (
        P("dp", "ctx", None),
        P(),
        P(("dp", "ctx"), None, None),
        P(("dp", "ctx"), None, None),
    )
    out_specs = P("dp", "ctx", None)
    body = functools.partial(shards, mesh.shape["dp"], mesh.shape["ctx"])
    return jax.shard_map(body, mesh=mesh, in_specs=in_specs, out_specs=out_specs, check_vma=False)
```
